256 devices in a mesh: depth: 4 (over y), cols: 64 (over z, x, core).
Axes of the slice: x: 4, y: 4, z: 8, core: 2. Of those that a mesh axis runs over, the one named last changes fastest.
Arguments:
- bricks: bfloat16 [4, 256, 256, 512], P('depth', 'cols'), may hold values from -6 to 6
- brick_owner: int32 [4, 65536, 1], P('depth', 'cols'), may hold values from 0 to 63; in each aligned block of 1024 rows (0 to 1023, 1024 to 2047, ..., all dimensions but the last counted through in order) at most 32 rows name the same one
- brick_slot: int32 [4, 65536], P('depth', 'cols'), may hold values from 0 to 3
- sample_base: int32 [4, 16, 65536], P('depth', None, 'cols'), may hold values from 0 to 3374
- corner_weights: bfloat16 [4, 8, 16, 65536], P('depth', None, None, 'cols'), may hold values from 0 to 1
- spacing: bfloat16 [4, 16, 65536], P('depth', None, 'cols'), may hold values from 0.029907227 to 0.079589844
- w_in: bfloat16 [128, 32], replicated, may hold values from -1 to 1
- w_mid: bfloat16 [128, 128], replicated, may hold values from -0.5 to 0.5
- w_last: bfloat16 [128, 128], replicated, may hold values from -0.5 to 0.5
- w_feat: bfloat16 [128, 128], replicated, may hold values from -0.5 to 0.5
- w_density: bfloat16 [1, 128], replicated, may hold values from -0.5 to 0.5
Outputs:
- image: float32 [128, 65536], P('depth', 'cols')
- visibility: float32 [4, 65536], P('depth', 'cols')
The draws below stay inside these ranges and needn't reach their ends.
Inputs may be any that keep to these rules, and one draw needn't show every extreme that they name: `brick_owner`: within each region, among the 1024 rays of one index of cols, at most 32 name the same owner, a bound that some block reaches of them. `sample_base`: the cell i * 15**2 + j * 15 + k with i, j, k below 15.
All inputs are finite; a program needn't handle non-finite values.
Results may differ from the reference program's by a relative error of at most 0.0019.
Values may be sent and summed in bfloat16 or wider, within the bound.
A program may use at most 128 MiB of HBM per device.

```python
import math
import jax
import jax.numpy as jnp
import numpy as np
from jax import lax

C = 32
EDGE = 16
S = 16
HID = 128
FEAT = 128
RAY_DEV = 1024
BR_DEV = 4
REGIONS = 4
RAYS = 65536
NB = 256
CAP = 32
N_COLS = 64


def plant(entries, key, low, top_value):
    index_at = [jax.random.randint(jax.random.fold_in(key, axis), (), 0, length) for axis, length in enumerate(entries.shape)]
    longest = entries.shape.index(max(entries.shape))
    neighbour = index_at[:longest] + [(index_at[longest] + 1) % entries.shape[longest]] + index_at[longest + 1:]
    return entries.at[tuple(index_at)].set(low).at[tuple(neighbour)].set(top_value)


def block_scale(stream_key, shape, cuts, low, top_value):
    def one(axis_at, blocks):
        heights = jax.random.uniform(jax.random.fold_in(jax.random.fold_in(stream_key, 6), axis_at), (blocks,), jnp.float32, low / len(cuts), top_value / len(cuts))
        return jnp.repeat(jnp.exp(heights), shape[axis_at] // blocks).reshape((-1,) + (1,) * (len(shape) - axis_at - 1))

    gain = one(*cuts[0])
    for cut in cuts[1:]:
        gain = gain * one(*cut)
    return gain


def deal_out(key, own, number, rows, count, top, reach, lean):
    sequence = jax.random.permutation(key, count)
    heavy_load, usual = portions_of(count, rows * top, reach, lean, True), portions_of(count, rows * top, reach, lean, False)
    places = jnp.arange(count)

    def named(sizes, turn):
        used = int((sizes > 0).sum())
        fixed = max(1, used // 4)
        passed = fixed + (places - fixed + turn * (used - fixed)) % max(1, count - fixed)
        return jnp.zeros((count,), jnp.int32).at[sequence[jnp.where(places < fixed, places, passed)]].set(jnp.asarray(sizes, jnp.int32))

    sizes = jnp.where(number % 4 == 0, named(heavy_load, number // 4), named(usual, number - number // 4 - 1))
    mixed = jax.random.permutation(jax.random.fold_in(own, 3), count)
    donor, taker = mixed[0:count // 2 * 2:2], mixed[1:count // 2 * 2:2]
    slack = jnp.minimum(sizes[donor] - 1, reach - sizes[taker]) // 2
    slack = jnp.where((donor == sequence[0]) | (taker == sequence[0]) | (sizes[taker] == 0), 0, jnp.maximum(slack, 0))
    passed = jax.random.randint(jax.random.fold_in(own, 4), (count // 2,), 0, 1 << 20) % (slack + 1)
    sizes = sizes.at[donor].add(-passed).at[taker].add(passed)
    members = jnp.searchsorted(jnp.cumsum(sizes), jnp.arange(rows * top), side="right").astype(jnp.int32)
    listing = members.reshape(top, rows).T
    listing = listing[jax.random.permutation(jax.random.fold_in(own, 1), rows)]
    turn = jax.random.randint(jax.random.fold_in(own, 2), (rows, 1), 0, top)
    return jnp.take_along_axis(listing, (jnp.arange(top)[None, :] + turn) % top, axis=1)


def portions_of(amount, total, bound, lean, full):
    loads = [(1 << 20) // math.isqrt(rank ** lean) + 1 for rank in range(1, amount + 1)]
    largest = bound if full else min(bound, max(-(-total // amount), total * loads[0] // sum(loads)))
    least = 1 if total - largest >= amount - 1 else 0
    counts, spare = [largest] + [least] * (amount - 1), total - largest - least * (amount - 1)
    while spare > 0:
        candidates = [i for i in range(1, amount) if counts[i] < largest] or [i for i in range(1, amount) if counts[i] < bound]
        mass, budget = sum([loads[i] for i in candidates]), spare
        for i in candidates:
            extra = min(bound - counts[i], max(1, budget * loads[i] // mass), spare)
            counts[i] = counts[i] + extra
            spare = spare - extra
    return np.array(counts)


def gaussian(own_key, shape, width, bound, cuts=(), kind=jnp.bfloat16):
    gain = block_scale(own_key, shape, cuts, -0.22, 0.18) if cuts else 1.0
    array = jax.random.normal(own_key, shape, jnp.float32) * width * gain
    return jnp.minimum(jnp.maximum(array, -bound), bound).astype(kind)


def setup_inputs(seed: int = 0) -> dict:
    arg_keys = jax.random.split(jax.random.key(seed), 12)
    bricks = gaussian(arg_keys[0], (REGIONS, NB, EDGE * EDGE, EDGE * C), 1.0, 6.0, ((0, 4), (1, 64)))
    brick_owner_keys = jax.random.split(jax.random.fold_in(arg_keys[1], 1), REGIONS * RAYS // RAY_DEV)
    brick_owner_turns = jax.random.permutation(jax.random.fold_in(arg_keys[1], 3), REGIONS * RAYS // RAY_DEV)
    brick_owner = jax.vmap(lambda own, number: deal_out(jax.random.fold_in(arg_keys[1], 2), own, number, RAY_DEV, N_COLS, 1, CAP, 2))(brick_owner_keys, brick_owner_turns).reshape((REGIONS, RAYS, 1))
    brick_slot = plant(jax.random.randint(arg_keys[2], (REGIONS, RAYS), 0, BR_DEV), jax.random.fold_in(arg_keys[2], 1), 0, BR_DEV - 1).astype(jnp.int32)
    sample_base = plant(jax.random.randint(arg_keys[3], (REGIONS, S, RAYS), 0, (EDGE - 1) ** 3), jax.random.fold_in(arg_keys[3], 1), 0, ((EDGE - 1) ** 3) - 1).astype(jnp.int32)
    corner_weights = jnp.clip(1.0 * jax.random.uniform(arg_keys[4], (REGIONS, 8, S, RAYS), jnp.float32) ** block_scale(arg_keys[4], (REGIONS, 8, S, RAYS), ((0, 4), (3, 64)), -0.2, 0.2), 0.0, 1.0).astype(jnp.bfloat16)
    spacing = jnp.clip(jnp.exp(math.log(0.079589844) - 0.97878635 * jax.random.uniform(arg_keys[5], (REGIONS, S, RAYS), jnp.float32) ** block_scale(arg_keys[5], (REGIONS, S, RAYS), ((0, 4), (2, 64)), -0.2, 0.2)), 0.029907227, 0.079589844).astype(jnp.bfloat16)
    w_in = gaussian(arg_keys[6], (HID, C), C ** -0.5, 1.0)
    w_mid = gaussian(arg_keys[7], (HID, HID), HID ** -0.5, 0.5)
    w_last = gaussian(arg_keys[8], (HID, HID), HID ** -0.5, 0.5)
    w_feat = gaussian(arg_keys[9], (FEAT, HID), HID ** -0.5, 0.5)
    w_density = gaussian(arg_keys[10], (1, HID), HID ** -0.5, 0.5)
    return {"bricks": bricks, "brick_owner": brick_owner, "brick_slot": brick_slot, "sample_base": sample_base, "corner_weights": corner_weights, "spacing": spacing, "w_in": w_in, "w_mid": w_mid, "w_last": w_last, "w_feat": w_feat, "w_density": w_density}


def interpolate(flat_voxels, brick_index, base_cell, weights, edge_cells):
    cell_side = edge_cells - 1
    coord_x = base_cell // (cell_side * cell_side)
    coord_y = (base_cell // cell_side) % cell_side
    coord_z = base_cell % cell_side
    samples, extent = base_cell.shape
    channels = flat_voxels.shape[1]
    total = jnp.zeros((samples, extent, channels), jnp.float32)
    for upper in range(2):
        for middle in range(2):
            for inner in range(2):
                corner = 4 * upper + 2 * middle + inner
                row_index = brick_index[None, :] * (edge_cells * edge_cells * edge_cells) + ((coord_x + upper) * edge_cells + (coord_y + middle)) * edge_cells + (coord_z + inner)
                gathered = jnp.take(flat_voxels, row_index.astype(jnp.int32), axis=0)
                total = total + gathered.astype(jnp.float32) * weights[corner].astype(jnp.float32)[:, :, None]
    return jnp.transpose(total, (2, 0, 1)).astype(jnp.bfloat16)


def shade(mixed_in, spacing_piece, w_in, w_mid, w_last, w_feat, w_density):
    channels, samples, extent = mixed_in.shape
    flat_in = mixed_in.reshape(channels, samples * extent)
    layer_one = jax.nn.relu(jnp.dot(w_in, flat_in, preferred_element_type=jnp.float32)).astype(jnp.bfloat16)
    layer_two = jax.nn.relu(jnp.dot(w_mid, layer_one, preferred_element_type=jnp.float32)).astype(jnp.bfloat16)
    layer_three = jax.nn.relu(jnp.dot(w_last, layer_two, preferred_element_type=jnp.float32)).astype(jnp.bfloat16)
    colour = jnp.dot(w_feat, layer_three, preferred_element_type=jnp.float32).reshape(-1, samples, extent)
    density = jax.nn.softplus(jnp.dot(w_density, layer_three, preferred_element_type=jnp.float32)).reshape(samples, extent)
    optical = density * spacing_piece.astype(jnp.float32)
    ahead_sum = jnp.cumsum(optical, axis=0) - optical
    weight = jnp.exp(-ahead_sum) * (-jnp.expm1(-optical))
    return jnp.sum(colour * weight[None], axis=1), jnp.sum(optical, axis=0)


def reference(bricks, brick_owner, brick_slot, sample_base, corner_weights, spacing, w_in, w_mid, w_last, w_feat, w_density):
    image = jnp.zeros((FEAT, RAYS), jnp.float32)
    before = jnp.zeros((RAYS,), jnp.float32)
    visible_rows = []
    for region in range(REGIONS):
        flat_voxels = bricks[region].reshape(NB * EDGE * EDGE * EDGE, C)
        brick_index = (brick_owner[region, :, 0] * BR_DEV + brick_slot[region]).astype(jnp.int32)
        bases = sample_base[region].astype(jnp.int32)
        weights = corner_weights[region]
        lengths = spacing[region]

        def group(group_index, flat_voxels=flat_voxels, brick_index=brick_index, bases=bases, weights=weights, lengths=lengths):
            group_start = (group_index * RAY_DEV).astype(jnp.int32)
            index_piece = lax.dynamic_slice_in_dim(brick_index, group_start, RAY_DEV, 0)
            base_piece = lax.dynamic_slice_in_dim(bases, group_start, RAY_DEV, 1)
            weight_piece = lax.dynamic_slice_in_dim(weights, group_start, RAY_DEV, 2)
            length_piece = lax.dynamic_slice_in_dim(lengths, group_start, RAY_DEV, 1)
            mixed_in = interpolate(flat_voxels, index_piece, base_piece, weight_piece, EDGE)
            return shade(mixed_in, length_piece, w_in, w_mid, w_last, w_feat, w_density)

        colour_groups, depth_groups = lax.map(group, jnp.arange(N_COLS, dtype=jnp.int32))
        region_colour = jnp.moveaxis(colour_groups, 0, 1).reshape(FEAT, RAYS)
        region_depth = depth_groups.reshape(RAYS)
        visible = jnp.exp(-before)
        visible_rows.append(visible)
        image = image + visible[None, :] * region_colour
        before = before + region_depth
    return image, jnp.stack(visible_rows, axis=0)
```

```python
import functools

import jax
import jax.numpy as jnp
from jax import lax
from jax.experimental import pallas as pl
from jax.experimental.pallas import tpu as pltpu
from jax.sharding import PartitionSpec as P

EDGE = 16
LINES = EDGE * EDGE
CH = 32
S = 16
HID = 128
COLS = 64
CAP = 32
HALF = CAP // 2
ROWS = 48
RAYS = 1024
SLOTS = COLS * CAP
TILE = 128
MAX_TILES = SLOTS // TILE + 3
POS = EDGE - 1
WIDE = 256
F32 = jnp.float32
BF16 = jnp.bfloat16


def iota(shape, dim, dtype=jnp.int32):
    return lax.broadcasted_iota(jnp.int32, shape, dim).astype(dtype)


def one_hot(mask):
    return jnp.where(mask, 1.0, 0.0).astype(BF16)


def dot(a, b):
    return jnp.dot(a, b, preferred_element_type=F32)


def dot_rows(a, b):
    return lax.dot_general(a, b, (((1,), (1,)), ((), ())), preferred_element_type=F32)


def ask_kernel(owner_ref, slot_ref, base_ref, weight_ref, spacing_ref, sent_ref, place_ref):
    owner = owner_ref[...]
    mine = iota((COLS, RAYS), 0) == owner
    earlier = one_hot(iota((RAYS, RAYS), 0) < iota((RAYS, RAYS), 1))
    count = dot(one_hot(mine), earlier)
    rank = jnp.sum(jnp.where(mine, count, 0.0), axis=0, keepdims=True).astype(jnp.int32)
    place = owner * CAP + rank
    place_ref[...] = place
    sent = dot_rows(one_hot(iota((SLOTS, RAYS), 0) == place), weight_ref[...])
    sent_ref[:, :CAP, :] = sent.astype(BF16).reshape(COLS, CAP, HID)
    base = base_ref[...].astype(F32) + 0.5
    side = EDGE - 1
    coord_x = jnp.floor(base * (1.0 / (side * side)))
    rest = base - coord_x * (side * side)
    coord_y = jnp.floor(rest * (1.0 / side))
    coord_z = rest - coord_y * side - 0.5
    line = coord_x * EDGE + coord_y
    slot = slot_ref[...].astype(F32) + 1.0
    slot_rows = jnp.where(iota((S, RAYS), 0) == 0, slot, 0.0)
    features = jnp.concatenate([line, coord_z, spacing_ref[...].astype(F32), slot_rows], axis=0)
    second = rank >= HALF
    both = jnp.concatenate(
        [jnp.where(second, 0.0, features), jnp.where(second, features, 0.0)], axis=0
    ).astype(BF16)
    row = owner * HALF + jnp.where(second, rank - HALF, rank)
    sent = dot_rows(one_hot(iota((COLS * HALF, RAYS), 0) == row), both)
    sent_ref[:, CAP:, :] = sent.astype(BF16).reshape(COLS, HALF, HID)


def field_kernel(
    got_ref,
    brick_ref,
    w_in_ref,
    w_mid_ref,
    w_last_ref,
    w_feat_ref,
    w_density_ref,
    colour_ref,
    depth_ref,
    table_ref,
    pos_ref,
    weight_ref,
    feature_ref,
    mix_ref,
    mixed_ref,
    hidden_ref,
    density_ref,
    reply_ref,
):
    half = COLS * HALF
    second = got_ref[:, CAP:, :].reshape(half, HID)
    lane = iota((half, HID), 1)
    table_ref[:half, :HID] = got_ref[:, :HALF, :].reshape(half, HID)
    table_ref[half:, :HID] = got_ref[:, HALF:CAP, :].reshape(half, HID)
    zero = jnp.zeros((half, HID), BF16)
    table_ref[:half, HID:] = jnp.where(lane < HID // 2, second, zero)
    table_ref[half:, HID:] = jnp.where(lane < HID // 2, zero, second)

    pick_row = iota((16, HID), 0)
    pick_lane = iota((16, HID), 1)
    picks = one_hot(pick_lane == jnp.where(pick_row < 2, 3 * S + pick_row * (HID // 2), -1))
    keys = dot_rows(picks, second)
    key = jnp.concatenate([keys[0:1], keys[1:2]], axis=1) - 1.0
    member = jnp.where(iota((8, SLOTS), 0, F32) == key, 1.0, 0.0)
    chunks = SLOTS // 128
    stacked = jnp.concatenate([member[:, c * 128 : (c + 1) * 128] for c in range(chunks)], axis=0)
    before = one_hot(iota((128, 128), 0) < iota((128, 128), 1))
    inner = dot(stacked.astype(BF16), before)
    totals = jnp.sum(stacked, axis=1, keepdims=True)
    carry = jnp.zeros((8, 1), F32)
    pieces = []
    for c in range(chunks):
        pieces.append(inner[c * 8 : (c + 1) * 8] + carry)
        carry = carry + totals[c * 8 : (c + 1) * 8]
    counted = jnp.concatenate(pieces, axis=1)
    tiles = jnp.floor((carry + (TILE - 1.0)) * (1.0 / TILE))
    row = iota((8, 1), 0)
    starts = [jnp.sum(jnp.where(row < q, tiles, 0.0)) for q in range(1, 5)]
    first = jnp.where(row == 1, starts[0], jnp.where(row == 2, starts[1], starts[2]))
    first = jnp.where(row == 0, 0.0, first)
    pos = jnp.sum(member * (counted + first * TILE), axis=0, keepdims=True)
    pos = jnp.where(jnp.sum(member, axis=0, keepdims=True) > 0.0, pos, -1.0)
    pos_ref[...] = jnp.broadcast_to(pos, (8, SLOTS))
    limit1, limit2, limit3, tile_count = [start.astype(jnp.int32) for start in starts]
    reply_ref[...] = jnp.zeros_like(reply_ref)

    def one_tile(tile, carried):
        brick = (
            (tile >= limit1).astype(jnp.int32)
            + (tile >= limit2).astype(jnp.int32)
            + (tile >= limit3).astype(jnp.int32)
        )
        local = pos_ref[0:1, :] - (tile * TILE).astype(F32)
        chosen = one_hot(iota((TILE, SLOTS), 0, F32) == local)
        rays = dot(chosen, table_ref[...]).T
        weight_ref[...] = rays[:HID]
        feature_ref[...] = rays[HID : HID + HID // 2] + rays[HID + HID // 2 :]

        for s in range(S):
            lanes = slice(s * TILE, (s + 1) * TILE)
            line = feature_ref[s : s + 1, :]
            coord_x = jnp.floor(line * (1.0 / EDGE))
            coord_y = line - coord_x * EDGE
            rows = iota((EDGE, TILE), 0, F32)
            near = rows == coord_y
            far = rows == coord_y + 1.0
            x_full = jnp.broadcast_to(coord_x, (EDGE, TILE)).astype(BF16)
            none = jnp.zeros((EDGE, TILE), BF16)
            for e in range(2):
                parts = []
                for a in range(2):
                    low = weight_ref[(4 * a + e) * S + s : (4 * a + e) * S + s + 1, :]
                    high = weight_ref[(4 * a + 2 + e) * S + s : (4 * a + 2 + e) * S + s + 1, :]
                    parts.append(jnp.where(near, low, jnp.where(far, high, 0.0)).astype(BF16))
                for x in range(EDGE):
                    value = jnp.where(x_full == x, parts[0], none)
                    if x > 0:
                        value = jnp.where(x_full == x - 1, parts[1], value)
                    mix_ref[e * LINES + x * EDGE : e * LINES + (x + 1) * EDGE, lanes] = value
        for group in range(S * TILE // WIDE):
            lanes = slice(group * WIDE, (group + 1) * WIDE)
            spread = dot(brick_ref[brick], mix_ref[:, lanes])
            each = WIDE // TILE
            coord_z = jnp.concatenate(
                [feature_ref[S + each * group + i : S + each * group + i + 1, :] for i in range(each)],
                axis=1,
            )
            mixed = jnp.zeros((CH, WIDE), F32)
            for p in range(POS):
                mixed = jnp.where(coord_z == float(p), spread[p * CH : (p + 1) * CH], mixed)
            mixed_ref[:, lanes] = mixed.astype(BF16)
        layer = mixed_ref[...]
        for w_ref in (w_in_ref, w_mid_ref, w_last_ref):
            layer = jnp.maximum(dot(w_ref[...], layer), 0.0).astype(BF16)
        hidden_ref[...] = layer
        thin = dot(w_density_ref[...], layer)
        for s in range(S):
            density_ref[s : s + 1, :] = thin[0:1, s * TILE : (s + 1) * TILE]

        density = density_ref[...]
        density = jnp.maximum(density, 0.0) + jnp.log1p(jnp.exp(-jnp.abs(density)))
        optical = density * feature_ref[2 * S : 3 * S, :]
        ahead = [jnp.zeros((1, TILE), F32)]
        for s in range(S):
            ahead.append(ahead[s] + optical[s : s + 1])
        clear = jnp.exp(-jnp.concatenate(ahead[:S], axis=0))
        share = clear * (1.0 - jnp.exp(-optical))
        total = jnp.zeros((HID, TILE), F32)
        for s in range(S):
            hidden = hidden_ref[:, s * TILE : (s + 1) * TILE].astype(F32)
            total = total + hidden * share[s : s + 1]
        high = total.astype(BF16)
        low = (total - high.astype(F32)).astype(BF16)
        colour = dot(w_feat_ref[...], high) + dot(w_feat_ref[...], low)
        thick = ahead[S]
        thick_high = thick.astype(BF16).astype(F32)
        thick_mid = (thick - thick_high).astype(BF16).astype(F32)
        thick_low = thick - thick_high - thick_mid
        extra = jnp.concatenate(
            [thick_high, thick_mid, thick_low, jnp.zeros((13, TILE), F32)], axis=0
        )
        result = jnp.concatenate([colour, extra], axis=0).astype(BF16)
        reply_ref[...] += dot(result, chosen)
        return carried

    lax.fori_loop(0, tile_count, one_tile, 0)
    for part in range(2):
        block = reply_ref[:HID, part * half : (part + 1) * half].T
        colour_ref[:, part * HALF : (part + 1) * HALF, :] = block.astype(BF16).reshape(
            COLS, HALF, HID
        )
    depth_ref[...] = reply_ref[HID : HID + 16, :].astype(BF16)


def collect_kernel(colour_ref, depth_ref, place_ref, out_ref):
    table = colour_ref[...].reshape(SLOTS, HID).astype(F32).T.astype(BF16)
    found = one_hot(iota((SLOTS, RAYS), 0) == place_ref[...])
    out_ref[:HID, :] = dot(table, found).astype(BF16)
    out_ref[HID:, :] = dot(depth_ref[...], found).astype(BF16)


def vmem(count):
    return [pl.BlockSpec(memory_space=pltpu.VMEM)] * count


def make_table(bricks):
    turned = jnp.transpose(bricks, (0, 2, 1))
    return jnp.concatenate([turned[:, : POS * CH], turned[:, CH:]], axis=2)


def run_field(got, table, w_in, w_mid, w_last, w_feat, w_density):
    return pl.pallas_call(
        field_kernel,
        out_shape=(
            jax.ShapeDtypeStruct((COLS, CAP, HID), BF16),
            jax.ShapeDtypeStruct((16, SLOTS), BF16),
        ),
        in_specs=vmem(7),
        out_specs=tuple(vmem(2)),
        scratch_shapes=[
            pltpu.VMEM((SLOTS, 2 * HID), BF16),
            pltpu.VMEM((8, SLOTS), F32),
            pltpu.VMEM((HID, TILE), F32),
            pltpu.VMEM((HID // 2, TILE), F32),
            pltpu.VMEM((2 * LINES, S * TILE), BF16),
            pltpu.VMEM((CH, S * TILE), BF16),
            pltpu.VMEM((HID, S * TILE), BF16),
            pltpu.VMEM((S, TILE), F32),
            pltpu.VMEM((HID + 16, SLOTS), F32),
        ],
        compiler_params=pltpu.CompilerParams(vmem_limit_bytes=48 << 20),
        name="field",
    )(got, table, w_in, w_mid, w_last, w_feat, jnp.pad(w_density, ((0, 15), (0, 0))))


def on_device(
    bricks,
    brick_owner,
    brick_slot,
    sample_base,
    corner_weights,
    spacing,
    w_in,
    w_mid,
    w_last,
    w_feat,
    w_density,
):
    params = pltpu.CompilerParams(vmem_limit_bytes=48 << 20)
    sent, place = pl.pallas_call(
        ask_kernel,
        out_shape=(
            jax.ShapeDtypeStruct((COLS, ROWS, HID), BF16),
            jax.ShapeDtypeStruct((1, RAYS), jnp.int32),
        ),
        in_specs=vmem(5),
        out_specs=tuple(vmem(2)),
        compiler_params=params,
        name="ask",
    )(
        brick_owner.reshape(1, RAYS),
        brick_slot,
        sample_base[0],
        corner_weights[0].reshape(HID, RAYS),
        spacing[0],
    )
    got = lax.all_to_all(sent, "cols", split_axis=0, concat_axis=0, tiled=True)
    table = make_table(bricks[0])
    colour, depth = run_field(got, table, w_in, w_mid, w_last, w_feat, w_density)
    return colour, depth, place


def finish(colour, depth, place):
    params = pltpu.CompilerParams(vmem_limit_bytes=48 << 20)
    depth = depth[:3].reshape(3, 2, COLS, HALF).transpose(2, 0, 1, 3).reshape(COLS, 3 * CAP)
    colour = lax.all_to_all(colour, "cols", split_axis=0, concat_axis=0, tiled=True)
    depth = lax.all_to_all(depth, "cols", split_axis=0, concat_axis=0, tiled=True)
    depth = depth.reshape(COLS, 3, CAP).transpose(1, 0, 2).reshape(3, SLOTS)
    depth = jnp.pad(depth, ((0, 13), (0, 0)))
    here = pl.pallas_call(
        collect_kernel,
        out_shape=jax.ShapeDtypeStruct((HID + 16, RAYS), BF16),
        in_specs=vmem(3),
        out_specs=vmem(1)[0],
        compiler_params=params,
        name="collect",
    )(colour, depth, place)
    regions = lax.axis_size("depth")
    rows = HID // regions
    out = jnp.concatenate(
        [
            here[:HID].reshape(regions, rows, RAYS),
            jnp.broadcast_to(here[HID:][None], (regions, 16, RAYS)),
        ],
        axis=1,
    )
    out = lax.all_to_all(out, "depth", split_axis=0, concat_axis=0, tiled=True)
    thick = jnp.sum(out[:, rows : rows + 3].astype(F32), axis=1)
    ahead = jnp.cumsum(thick, axis=0) - thick
    visible = jnp.exp(-ahead)
    image = jnp.sum(visible[:, None, :] * out[:, :rows].astype(F32), axis=0)
    me = lax.axis_index("depth")
    mine = jnp.sum(jnp.where(jnp.arange(regions)[:, None] == me, visible, 0.0), axis=0)
    return image, mine[None, :]


def whole(*args):
    return finish(*on_device(*args))


def solution(mesh):
    in_specs = (
        P("depth", "cols", None, None),
        P("depth", "cols", None),
        P("depth", "cols"),
        P("depth", None, "cols"),
        P("depth", None, None, "cols"),
        P("depth", None, "cols"),
        P(),
        P(),
        P(),
        P(),
        P(),
    )
    out_specs = (P("depth", "cols"), P("depth", "cols"))
    return jax.shard_map(
        whole, mesh=mesh, in_specs=in_specs, out_specs=out_specs, check_vma=False
    )
```

```python
import jax
import jax.numpy as jnp
from jax import lax
from jax.experimental import pallas as pl
from jax.experimental.pallas import tpu as pltpu
from jax.sharding import PartitionSpec as P

EDGE = 16
LINES = EDGE * EDGE
CH = 32
S = 16
HID = 128
COLS = 64
CAP = 32
HALF = CAP // 2
ROWS = 48
BACK = CAP + 8
RAYS = 1024
SLOTS = COLS * CAP
TILE = 128
MAX_TILES = SLOTS // TILE + 3
POS = EDGE - 1
WIDE = 256
F32 = jnp.float32
BF16 = jnp.bfloat16
MESH = pl.DeviceIdType.MESH


def iota(shape, dim, dtype=jnp.int32):
    return lax.broadcasted_iota(jnp.int32, shape, dim).astype(dtype)


def one_hot(mask):
    return jnp.where(mask, 1.0, 0.0).astype(BF16)


def dot(a, b):
    return jnp.dot(a, b, preferred_element_type=F32)


def dot_rows(a, b):
    return lax.dot_general(a, b, (((1,), (1,)), ((), ())), preferred_element_type=F32)


def greet(barrier, count):
    me = lax.axis_index("cols")

    def signal(step, carried):
        peer = lax.rem(me + step, count)
        pl.semaphore_signal(barrier, inc=1, device_id={"cols": peer}, device_id_type=MESH)
        return carried

    lax.fori_loop(1, count, signal, 0)


def exchange(from_ref, to_ref, send_sem, recv_sem, local_sem):
    me = lax.axis_index("cols")

    def send(step, carried):
        peer = lax.rem(me + step, COLS)
        pltpu.make_async_remote_copy(
            src_ref=from_ref.at[peer],
            dst_ref=to_ref.at[me],
            send_sem=send_sem,
            recv_sem=recv_sem,
            device_id={"cols": peer},
            device_id_type=MESH,
        ).start()
        return carried

    lax.fori_loop(1, COLS, send, 0)
    own = pltpu.make_async_copy(from_ref.at[me], to_ref.at[me], local_sem)
    own.start()
    own.wait()
    others = pl.ds(0, COLS - 1)
    pltpu.make_async_copy(from_ref.at[others], from_ref.at[others], send_sem).wait()
    pltpu.make_async_copy(to_ref.at[others], to_ref.at[others], recv_sem).wait()


def ask_kernel(
    owner_hbm,
    slot_hbm,
    base_hbm,
    weight_hbm,
    spacing_hbm,
    got_ref,
    place_ref,
    sent_ref,
    owner_ref,
    slot_ref,
    base_ref,
    weight_ref,
    spacing_ref,
    load_sem,
    send_sem,
    recv_sem,
    local_sem,
):
    loads = [
        pltpu.make_async_copy(source, target, load_sem.at[i])
        for i, (source, target) in enumerate(
            (
                (owner_hbm, owner_ref),
                (slot_hbm, slot_ref),
                (base_hbm, base_ref),
                (weight_hbm, weight_ref),
                (spacing_hbm, spacing_ref),
            )
        )
    ]
    for load in loads:
        load.start()
    barrier = pltpu.get_barrier_semaphore()
    greet(barrier, COLS)
    for load in loads:
        load.wait()
    owner = owner_ref[...]
    mine = iota((COLS, RAYS), 0) == owner
    earlier = one_hot(iota((RAYS, RAYS), 0) < iota((RAYS, RAYS), 1))
    count = dot(one_hot(mine), earlier)
    rank = jnp.sum(jnp.where(mine, count, 0.0), axis=0, keepdims=True).astype(jnp.int32)
    place = owner * CAP + rank
    place_ref[...] = jnp.concatenate([owner, rank], axis=0)
    sent = dot_rows(one_hot(iota((SLOTS, RAYS), 0) == place), weight_ref[...])
    sent_ref[:, :CAP, :] = sent.astype(BF16).reshape(COLS, CAP, HID)
    base = base_ref[...].astype(F32) + 0.5
    side = EDGE - 1
    coord_x = jnp.floor(base * (1.0 / (side * side)))
    rest = base - coord_x * (side * side)
    coord_y = jnp.floor(rest * (1.0 / side))
    coord_z = rest - coord_y * side - 0.5
    line = coord_x * EDGE + coord_y
    slot = slot_ref[...].astype(F32) + 1.0
    slot_rows = jnp.where(iota((S, RAYS), 0) == 0, slot, 0.0)
    features = jnp.concatenate([line, coord_z, spacing_ref[...].astype(F32), slot_rows], axis=0)
    second = rank >= HALF
    both = jnp.concatenate(
        [jnp.where(second, 0.0, features), jnp.where(second, features, 0.0)], axis=0
    ).astype(BF16)
    row = owner * HALF + jnp.where(second, rank - HALF, rank)
    sent = dot_rows(one_hot(iota((COLS * HALF, RAYS), 0) == row), both)
    sent_ref[:, CAP:, :] = sent.astype(BF16).reshape(COLS, HALF, HID)
    pl.semaphore_wait(barrier, COLS - 1)
    exchange(sent_ref, got_ref, send_sem, recv_sem, local_sem)


def field_kernel(
    got_ref,
    brick_ref,
    w_in_ref,
    w_mid_ref,
    w_last_ref,
    w_feat_ref,
    w_density_ref,
    block_ref,
    table_ref,
    pos_ref,
    weight_ref,
    feature_ref,
    mix_ref,
    mixed_ref,
    hidden_ref,
    density_ref,
    reply_ref,
):
    half = COLS * HALF
    second = got_ref[:, CAP:, :].reshape(half, HID)
    lane = iota((half, HID), 1)
    table_ref[:half, :HID] = got_ref[:, :HALF, :].reshape(half, HID)
    table_ref[half:, :HID] = got_ref[:, HALF:CAP, :].reshape(half, HID)
    zero = jnp.zeros((half, HID), BF16)
    table_ref[:half, HID:] = jnp.where(lane < HID // 2, second, zero)
    table_ref[half:, HID:] = jnp.where(lane < HID // 2, zero, second)

    pick_row = iota((16, HID), 0)
    pick_lane = iota((16, HID), 1)
    picks = one_hot(pick_lane == jnp.where(pick_row < 2, 3 * S + pick_row * (HID // 2), -1))
    keys = dot_rows(picks, second)
    key = jnp.concatenate([keys[0:1], keys[1:2]], axis=1) - 1.0
    member = jnp.where(iota((8, SLOTS), 0, F32) == key, 1.0, 0.0)
    chunks = SLOTS // 128
    stacked = jnp.concatenate([member[:, c * 128 : (c + 1) * 128] for c in range(chunks)], axis=0)
    before = one_hot(iota((128, 128), 0) < iota((128, 128), 1))
    inner = dot(stacked.astype(BF16), before)
    totals = jnp.sum(stacked, axis=1, keepdims=True)
    carry = jnp.zeros((8, 1), F32)
    pieces = []
    for c in range(chunks):
        pieces.append(inner[c * 8 : (c + 1) * 8] + carry)
        carry = carry + totals[c * 8 : (c + 1) * 8]
    counted = jnp.concatenate(pieces, axis=1)
    tiles = jnp.floor((carry + (TILE - 1.0)) * (1.0 / TILE))
    row = iota((8, 1), 0)
    starts = [jnp.sum(jnp.where(row < q, tiles, 0.0)) for q in range(1, 5)]
    first = jnp.where(row == 1, starts[0], jnp.where(row == 2, starts[1], starts[2]))
    first = jnp.where(row == 0, 0.0, first)
    pos = jnp.sum(member * (counted + first * TILE), axis=0, keepdims=True)
    pos = jnp.where(jnp.sum(member, axis=0, keepdims=True) > 0.0, pos, -1.0)
    pos_ref[...] = jnp.broadcast_to(pos, (8, SLOTS))
    limit1, limit2, limit3, tile_count = [start.astype(jnp.int32) for start in starts]
    reply_ref[...] = jnp.zeros_like(reply_ref)

    def one_tile(tile, carried):
        brick = (
            (tile >= limit1).astype(jnp.int32)
            + (tile >= limit2).astype(jnp.int32)
            + (tile >= limit3).astype(jnp.int32)
        )
        local = pos_ref[0:1, :] - (tile * TILE).astype(F32)
        chosen = one_hot(iota((TILE, SLOTS), 0, F32) == local)
        rays = dot(chosen, table_ref[...]).T
        weight_ref[...] = rays[:HID]
        feature_ref[...] = rays[HID : HID + HID // 2] + rays[HID + HID // 2 :]

        for s in range(S):
            lanes = slice(s * TILE, (s + 1) * TILE)
            line = feature_ref[s : s + 1, :]
            coord_x = jnp.floor(line * (1.0 / EDGE))
            coord_y = line - coord_x * EDGE
            rows = iota((EDGE, TILE), 0, F32)
            near = rows == coord_y
            far = rows == coord_y + 1.0
            x_full = jnp.broadcast_to(coord_x, (EDGE, TILE)).astype(BF16)
            none = jnp.zeros((EDGE, TILE), BF16)
            for e in range(2):
                parts = []
                for a in range(2):
                    low = weight_ref[(4 * a + e) * S + s : (4 * a + e) * S + s + 1, :]
                    high = weight_ref[(4 * a + 2 + e) * S + s : (4 * a + 2 + e) * S + s + 1, :]
                    parts.append(jnp.where(near, low, jnp.where(far, high, 0.0)).astype(BF16))
                for x in range(EDGE):
                    value = jnp.where(x_full == x, parts[0], none)
                    if x > 0:
                        value = jnp.where(x_full == x - 1, parts[1], value)
                    mix_ref[e * LINES + x * EDGE : e * LINES + (x + 1) * EDGE, lanes] = value
        for group in range(S * TILE // WIDE):
            lanes = slice(group * WIDE, (group + 1) * WIDE)
            spread = dot(brick_ref[brick], mix_ref[:, lanes])
            each = WIDE // TILE
            coord_z = jnp.concatenate(
                [feature_ref[S + each * group + i : S + each * group + i + 1, :] for i in range(each)],
                axis=1,
            )
            mixed = jnp.zeros((CH, WIDE), F32)
            for p in range(POS):
                mixed = jnp.where(coord_z == float(p), spread[p * CH : (p + 1) * CH], mixed)
            mixed_ref[:, lanes] = mixed.astype(BF16)
        layer = mixed_ref[...]
        for w_ref in (w_in_ref, w_mid_ref, w_last_ref):
            layer = jnp.maximum(dot(w_ref[...], layer), 0.0).astype(BF16)
        hidden_ref[...] = layer
        thin = dot(w_density_ref[...], layer)
        for s in range(S):
            density_ref[s : s + 1, :] = thin[0:1, s * TILE : (s + 1) * TILE]

        density = density_ref[...]
        density = jnp.maximum(density, 0.0) + jnp.log1p(jnp.exp(-jnp.abs(density)))
        optical = density * feature_ref[2 * S : 3 * S, :]
        ahead = [jnp.zeros((1, TILE), F32)]
        for s in range(S):
            ahead.append(ahead[s] + optical[s : s + 1])
        clear = jnp.exp(-jnp.concatenate(ahead[:S], axis=0))
        share = clear * (1.0 - jnp.exp(-optical))
        total = jnp.zeros((HID, TILE), F32)
        for s in range(S):
            hidden = hidden_ref[:, s * TILE : (s + 1) * TILE].astype(F32)
            total = total + hidden * share[s : s + 1]
        high = total.astype(BF16)
        low = (total - high.astype(F32)).astype(BF16)
        colour = dot(w_feat_ref[...], high) + dot(w_feat_ref[...], low)
        thick = ahead[S]
        thick_high = thick.astype(BF16).astype(F32)
        thick_mid = (thick - thick_high).astype(BF16).astype(F32)
        thick_low = thick - thick_high - thick_mid
        extra = jnp.concatenate(
            [thick_high, thick_mid, thick_low, jnp.zeros((13, TILE), F32)], axis=0
        )
        result = jnp.concatenate([colour, extra], axis=0).astype(BF16)
        reply_ref[...] += dot(result, chosen)
        return carried

    lax.fori_loop(0, tile_count, one_tile, 0)
    for part in range(2):
        block = reply_ref[:HID, part * half : (part + 1) * half].T
        block_ref[:, part * HALF : (part + 1) * HALF, :] = block.astype(BF16).reshape(
            COLS, HALF, HID
        )
    index = iota((1, SLOTS), 1, F32)
    part = jnp.floor(index * (1.0 / half))
    inside = index - part * half
    column = jnp.floor(inside * (1.0 / HALF))
    rank = inside - column * HALF + part * HALF
    columns = one_hot(iota((COLS, SLOTS), 0, F32) == column)
    ranks = iota((CAP, SLOTS), 0, F32) == rank
    spots = jnp.concatenate(
        [jnp.where(ranks, reply_ref[HID + i : HID + i + 1, :], 0.0) for i in range(4)], axis=0
    ).astype(BF16)
    depth = dot_rows(columns, spots)
    block_ref[:, CAP:, :] = jnp.broadcast_to(depth.reshape(COLS, 1, HID), (COLS, 8, HID)).astype(BF16)


def collect_kernel(
    block_ref,
    place_ref,
    image_ref,
    visible_ref,
    got_ref,
    here_ref,
    thick_ref,
    colours_ref,
    thicks_ref,
    send_sem,
    recv_sem,
    local_sem,
    colour_send,
    colour_recv,
    thick_send,
    thick_recv,
):
    regions = lax.axis_size("depth")
    me = lax.axis_index("depth")
    barrier = pltpu.get_barrier_semaphore()
    greet(barrier, COLS)
    for step in range(1, regions):
        peer = lax.rem(me + step, regions)
        pl.semaphore_signal(barrier, inc=1, device_id={"depth": peer}, device_id_type=MESH)
    owner = place_ref[0:1, :]
    rank = place_ref[1:2, :]
    pl.semaphore_wait(barrier, COLS - 1 + regions - 1)
    exchange(block_ref, got_ref, send_sem, recv_sem, local_sem)
    mine = one_hot(iota((COLS, RAYS), 0) == owner)
    depth = jnp.max(got_ref[:, CAP:, :].astype(F32), axis=1)
    depth = dot(depth.T.astype(BF16), mine)
    ranks = iota((CAP, RAYS), 0) == rank
    thick = jnp.zeros((1, RAYS), F32)
    for i in range(3):
        piece = jnp.where(ranks, depth[i * CAP : (i + 1) * CAP], 0.0)
        thick = thick + jnp.sum(piece, axis=0, keepdims=True)
    thick_ref[...] = thick
    copies = []
    for step in range(1, regions):
        peer = lax.rem(me + step, regions)
        copy = pltpu.make_async_remote_copy(
            src_ref=thick_ref,
            dst_ref=thicks_ref.at[step],
            send_sem=thick_send.at[step],
            recv_sem=thick_recv.at[step],
            device_id={"depth": peer},
            device_id_type=MESH,
        )
        copy.start()
        copies.append(copy)
    table = got_ref[:, :CAP, :].reshape(SLOTS, HID).astype(F32).T.astype(BF16)
    found = one_hot(iota((SLOTS, RAYS), 0) == owner * CAP + rank)
    rows = HID // regions
    here_ref[...] = dot(table, found).astype(BF16).reshape(regions, rows, RAYS)
    for step in range(1, regions):
        peer = lax.rem(me + step, regions)
        copy = pltpu.make_async_remote_copy(
            src_ref=here_ref.at[peer],
            dst_ref=colours_ref.at[step],
            send_sem=colour_send.at[step],
            recv_sem=colour_recv.at[step],
            device_id={"depth": peer},
            device_id_type=MESH,
        )
        copy.start()
        copies.append(copy)
    for copy in copies:
        copy.wait()
    parts = [thick] + [thicks_ref[step] for step in range(1, regions)]
    sources = [lax.rem(me - step + regions, regions) for step in range(regions)]
    image = jnp.zeros((rows, RAYS), F32)
    for step in range(regions):
        ahead = jnp.zeros((1, RAYS), F32)
        for other in range(regions):
            if other != step:
                front = (sources[other] < sources[step]).astype(F32)
                ahead = ahead + front * parts[other]
        visible = jnp.exp(-ahead)
        if step == 0:
            visible_ref[...] = visible
            colour = here_ref[me]
        else:
            colour = colours_ref[step]
        image = image + visible * colour.astype(F32)
    image_ref[...] = image


def vmem(count):
    return [pl.BlockSpec(memory_space=pltpu.VMEM)] * count


def make_table(bricks):
    turned = jnp.transpose(bricks, (0, 2, 1))
    return jnp.concatenate([turned[:, : POS * CH], turned[:, CH:]], axis=2)


def run_field(got, table, w_in, w_mid, w_last, w_feat, w_density):
    return pl.pallas_call(
        field_kernel,
        out_shape=jax.ShapeDtypeStruct((COLS, BACK, HID), BF16),
        in_specs=vmem(7),
        out_specs=vmem(1)[0],
        scratch_shapes=[
            pltpu.VMEM((SLOTS, 2 * HID), BF16),
            pltpu.VMEM((8, SLOTS), F32),
            pltpu.VMEM((HID, TILE), F32),
            pltpu.VMEM((HID // 2, TILE), F32),
            pltpu.VMEM((2 * LINES, S * TILE), BF16),
            pltpu.VMEM((CH, S * TILE), BF16),
            pltpu.VMEM((HID, S * TILE), BF16),
            pltpu.VMEM((S, TILE), F32),
            pltpu.VMEM((HID + 16, SLOTS), F32),
        ],
        compiler_params=pltpu.CompilerParams(vmem_limit_bytes=48 << 20),
        name="field",
    )(got, table, w_in, w_mid, w_last, w_feat, jnp.pad(w_density, ((0, 15), (0, 0))))


def on_device(
    bricks,
    brick_owner,
    brick_slot,
    sample_base,
    corner_weights,
    spacing,
    w_in,
    w_mid,
    w_last,
    w_feat,
    w_density,
):
    got, place = pl.pallas_call(
        ask_kernel,
        out_shape=(
            jax.ShapeDtypeStruct((COLS, ROWS, HID), BF16),
            jax.ShapeDtypeStruct((2, RAYS), jnp.int32),
        ),
        in_specs=[pl.BlockSpec(memory_space=pl.ANY)] * 5,
        out_specs=tuple(vmem(2)),
        scratch_shapes=[
            pltpu.VMEM((COLS, ROWS, HID), BF16),
            pltpu.VMEM((1, RAYS), jnp.int32),
            pltpu.VMEM((1, RAYS), jnp.int32),
            pltpu.VMEM((S, RAYS), jnp.int32),
            pltpu.VMEM((HID, RAYS), BF16),
            pltpu.VMEM((S, RAYS), BF16),
            pltpu.SemaphoreType.DMA((5,)),
            pltpu.SemaphoreType.DMA,
            pltpu.SemaphoreType.DMA,
            pltpu.SemaphoreType.DMA,
        ],
        compiler_params=pltpu.CompilerParams(
            vmem_limit_bytes=32 << 20, collective_id=0, has_side_effects=True
        ),
        name="ask",
    )(
        brick_owner.reshape(1, RAYS),
        brick_slot,
        sample_base[0],
        corner_weights[0].reshape(HID, RAYS),
        spacing[0],
    )
    table = make_table(bricks[0])
    block = run_field(got, table, w_in, w_mid, w_last, w_feat, w_density)
    regions = lax.axis_size("depth")
    rows = HID // regions
    return pl.pallas_call(
        collect_kernel,
        out_shape=(
            jax.ShapeDtypeStruct((rows, RAYS), F32),
            jax.ShapeDtypeStruct((1, RAYS), F32),
        ),
        in_specs=vmem(2),
        out_specs=tuple(vmem(2)),
        scratch_shapes=[
            pltpu.VMEM((COLS, BACK, HID), BF16),
            pltpu.VMEM((regions, rows, RAYS), BF16),
            pltpu.VMEM((1, RAYS), F32),
            pltpu.VMEM((regions, rows, RAYS), BF16),
            pltpu.VMEM((regions, 1, RAYS), F32),
            pltpu.SemaphoreType.DMA,
            pltpu.SemaphoreType.DMA,
            pltpu.SemaphoreType.DMA,
            pltpu.SemaphoreType.DMA((regions,)),
            pltpu.SemaphoreType.DMA((regions,)),
            pltpu.SemaphoreType.DMA((regions,)),
            pltpu.SemaphoreType.DMA((regions,)),
        ],
        compiler_params=pltpu.CompilerParams(
            vmem_limit_bytes=32 << 20, collective_id=1, has_side_effects=True
        ),
        name="collect",
    )(block, place)


def solution(mesh):
    in_specs = (
        P("depth", "cols", None, None),
        P("depth", "cols", None),
        P("depth", "cols"),
        P("depth", None, "cols"),
        P("depth", None, None, "cols"),
        P("depth", None, "cols"),
        P(),
        P(),
        P(),
        P(),
        P(),
    )
    out_specs = (P("depth", "cols"), P("depth", "cols"))
    return jax.shard_map(
        on_device, mesh=mesh, in_specs=in_specs, out_specs=out_specs, check_vma=False
    )
```

```python
import jax
import jax.numpy as jnp
from jax import lax
from jax.experimental import pallas as pl
from jax.experimental.pallas import tpu as pltpu
from jax.sharding import PartitionSpec as P

EDGE = 16
LINES = EDGE * EDGE
CH = 32
S = 16
HID = 128
COLS = 64
CAP = 32
HALF = CAP // 2
ROWS = 48
RAYS = 1024
SLOTS = COLS * CAP
TILE = 128
MAX_TILES = SLOTS // TILE + 3
POS = EDGE - 1
WIDE = 256
EACH = WIDE // TILE
GATHER = 4
SPACE = MAX_TILES + 1
BUFFERS = 2
F32 = jnp.float32
BF16 = jnp.bfloat16
MESH = pl.DeviceIdType.MESH


def iota(shape, dim, dtype=jnp.int32):
    return lax.broadcasted_iota(jnp.int32, shape, dim).astype(dtype)


def one_hot(mask):
    return jnp.where(mask, 1.0, 0.0).astype(BF16)


def dot(a, b):
    return jnp.dot(a, b, preferred_element_type=F32)


def dot_rows(a, b):
    return lax.dot_general(a, b, (((1,), (1,)), ((), ())), preferred_element_type=F32)


def greet(barrier, count):
    me = lax.axis_index("cols")

    def signal(step, carried):
        peer = lax.rem(me + step, count)
        pl.semaphore_signal(barrier, inc=1, device_id={"cols": peer}, device_id_type=MESH)
        return carried

    lax.fori_loop(1, count, signal, 0)


def start_exchange(from_ref, to_ref, send_sem, recv_sem, local_sem):
    me = lax.axis_index("cols")

    def send(step, carried):
        peer = lax.rem(me + step, COLS)
        pltpu.make_async_remote_copy(
            src_ref=from_ref.at[peer],
            dst_ref=to_ref.at[me],
            send_sem=send_sem,
            recv_sem=recv_sem,
            device_id={"cols": peer},
            device_id_type=MESH,
        ).start()
        return carried

    lax.fori_loop(1, COLS, send, 0)
    pltpu.make_async_copy(from_ref.at[me], to_ref.at[me], local_sem).start()


def end_exchange(from_ref, to_ref, send_sem, recv_sem, local_sem):
    me = lax.axis_index("cols")
    others = pl.ds(0, COLS - 1)
    pltpu.make_async_copy(from_ref.at[me], to_ref.at[me], local_sem).wait()
    pltpu.make_async_copy(from_ref.at[others], from_ref.at[others], send_sem).wait()
    pltpu.make_async_copy(to_ref.at[others], to_ref.at[others], recv_sem).wait()


def ask_kernel(
    owner_hbm,
    slot_hbm,
    base_hbm,
    weight_hbm,
    spacing_hbm,
    brick_hbm,
    got_ref,
    place_ref,
    table_hbm,
    sent_ref,
    owner_ref,
    slot_ref,
    base_ref,
    weight_ref,
    spacing_ref,
    brick_ref,
    table_ref,
    load_sem,
    table_sem,
    send_sem,
    recv_sem,
    local_sem,
):
    loads = [
        pltpu.make_async_copy(source, target, load_sem.at[i])
        for i, (source, target) in enumerate(
            (
                (owner_hbm, owner_ref),
                (slot_hbm, slot_ref),
                (base_hbm, base_ref),
                (weight_hbm, weight_ref),
                (spacing_hbm, spacing_ref),
                (brick_hbm, brick_ref),
            )
        )
    ]
    for load in loads:
        load.start()
    barrier = pltpu.get_barrier_semaphore()
    greet(barrier, COLS)
    for load in loads[:5]:
        load.wait()
    owner = owner_ref[...]
    mine = iota((COLS, RAYS), 0) == owner
    earlier = one_hot(iota((RAYS, RAYS), 0) < iota((RAYS, RAYS), 1))
    count = dot(one_hot(mine), earlier)
    rank = jnp.sum(jnp.where(mine, count, 0.0), axis=0, keepdims=True).astype(jnp.int32)
    place = owner * CAP + rank
    place_ref[...] = jnp.concatenate([owner, rank], axis=0)
    sent = dot_rows(one_hot(iota((SLOTS, RAYS), 0) == place), weight_ref[...])
    sent_ref[:, :CAP, :] = sent.astype(BF16).reshape(COLS, CAP, HID)
    base = base_ref[...].astype(F32) + 0.5
    side = EDGE - 1
    coord_x = jnp.floor(base * (1.0 / (side * side)))
    rest = base - coord_x * (side * side)
    coord_y = jnp.floor(rest * (1.0 / side))
    coord_z = rest - coord_y * side - 0.5
    line = coord_x * EDGE + coord_y
    slot = slot_ref[...].astype(F32) + 1.0
    slot_rows = jnp.where(iota((S, RAYS), 0) == 0, slot, 0.0)
    features = jnp.concatenate([line, coord_z, spacing_ref[...].astype(F32), slot_rows], axis=0)
    second = rank >= HALF
    both = jnp.concatenate(
        [jnp.where(second, 0.0, features), jnp.where(second, features, 0.0)], axis=0
    ).astype(BF16)
    row = owner * HALF + jnp.where(second, rank - HALF, rank)
    sent = dot_rows(one_hot(iota((COLS * HALF, RAYS), 0) == row), both)
    sent_ref[:, CAP:, :] = sent.astype(BF16).reshape(COLS, HALF, HID)
    pl.semaphore_wait(barrier, COLS - 1)
    start_exchange(sent_ref, got_ref, send_sem, recv_sem, local_sem)
    loads[5].wait()
    for q in range(brick_ref.shape[0]):
        turned = brick_ref[q].astype(F32).T.astype(BF16)
        table_ref[q, :, :LINES] = turned[: POS * CH]
        table_ref[q, :, LINES:] = turned[CH:]
    store = pltpu.make_async_copy(table_ref, table_hbm, table_sem)
    store.start()
    store.wait()
    end_exchange(sent_ref, got_ref, send_sem, recv_sem, local_sem)


def field_kernel(
    got_hbm,
    brick_hbm,
    w_in_hbm,
    w_mid_hbm,
    w_last_hbm,
    w_feat_hbm,
    w_density_hbm,
    colour_ref,
    depth_ref,
    got_ref,
    brick_ref,
    turned_ref,
    w_in_ref,
    w_mid_ref,
    w_last_ref,
    w_feat_ref,
    thin_ref,
    w_density_ref,
    load_sem,
    table_ref,
    pos_ref,
    chosen_ref,
    weight_ref,
    feature_ref,
    mix_ref,
    mixed_ref,
    hidden_ref,
    density_ref,
    result_ref,
    reply_ref,
):
    loads = [
        pltpu.make_async_copy(source, target, load_sem.at[i])
        for i, (source, target) in enumerate(
            (
                (got_hbm, got_ref),
                (brick_hbm, brick_ref),
                (w_in_hbm, turned_ref),
                (w_mid_hbm, w_mid_ref),
                (w_last_hbm, w_last_ref),
                (w_feat_hbm, w_feat_ref),
                (w_density_hbm, thin_ref),
            )
        )
    ]
    for load in loads:
        load.start()
    loads[0].wait()
    half = COLS * HALF
    second = got_ref[:, CAP:, :].reshape(half, HID)
    lane = iota((half, HID), 1)
    table_ref[:half, :HID] = got_ref[:, :HALF, :].reshape(half, HID)
    table_ref[half:, :HID] = got_ref[:, HALF:CAP, :].reshape(half, HID)
    zero = jnp.zeros((half, HID), BF16)
    table_ref[:half, HID:] = jnp.where(lane < HID // 2, second, zero)
    table_ref[half:, HID:] = jnp.where(lane < HID // 2, zero, second)

    pick_row = iota((16, HID), 0)
    pick_lane = iota((16, HID), 1)
    picks = one_hot(pick_lane == jnp.where(pick_row < 2, 3 * S + pick_row * (HID // 2), -1))
    keys = dot_rows(picks, second)
    key = jnp.concatenate([keys[0:1], keys[1:2]], axis=1) - 1.0
    member = jnp.where(iota((8, SLOTS), 0, F32) == key, 1.0, 0.0)
    chunks = SLOTS // 128
    stacked = jnp.concatenate([member[:, c * 128 : (c + 1) * 128] for c in range(chunks)], axis=0)
    before = one_hot(iota((128, 128), 0) < iota((128, 128), 1))
    inner = dot(stacked.astype(BF16), before)
    totals = jnp.sum(stacked, axis=1, keepdims=True)
    carry = jnp.zeros((8, 1), F32)
    pieces = []
    for c in range(chunks):
        pieces.append(inner[c * 8 : (c + 1) * 8] + carry)
        carry = carry + totals[c * 8 : (c + 1) * 8]
    counted = jnp.concatenate(pieces, axis=1)
    tiles = jnp.floor((carry + (TILE - 1.0)) * (1.0 / TILE))
    row = iota((8, 1), 0)
    starts = [jnp.sum(jnp.where(row < q, tiles, 0.0)) for q in range(1, 5)]
    first = jnp.where(row == 1, starts[0], jnp.where(row == 2, starts[1], starts[2]))
    first = jnp.where(row == 0, 0.0, first)
    pos = jnp.sum(member * (counted + first * TILE), axis=0, keepdims=True)
    pos = jnp.where(jnp.sum(member, axis=0, keepdims=True) > 0.0, pos, -1.0)
    pos_ref[...] = jnp.broadcast_to(pos, (8, SLOTS))
    limit1, limit2, limit3, tile_count = [start.astype(jnp.int32) for start in starts]
    reply_ref[...] = jnp.zeros_like(reply_ref)
    result_ref[...] = jnp.zeros_like(result_ref)

    def gather(step, carried):
        for u in range(GATHER):
            tile = step * GATHER + u
            local = pos_ref[0:1, :] - (tile * TILE).astype(F32)
            chosen_ref[tile] = one_hot(iota((TILE, SLOTS), 0, F32) == local)
        chosen = chosen_ref[pl.ds(step * GATHER, GATHER)].reshape(GATHER * TILE, SLOTS)
        rays = dot(chosen, table_ref[...])
        for u in range(GATHER):
            turned = rays[u * TILE : (u + 1) * TILE].T
            weight_ref[step * GATHER + u] = turned[:HID]
            feature_ref[step * GATHER + u] = turned[HID : HID + HID // 2] + turned[HID + HID // 2 :]
        return carried

    lax.fori_loop(0, lax.div(tile_count + GATHER - 1, GATHER), gather, 0)

    def build(tile, u, s):
        lanes = slice(s * TILE, (s + 1) * TILE)
        line = feature_ref[tile, s : s + 1, :]
        coord_x = jnp.floor(line * (1.0 / EDGE))
        coord_y = line - coord_x * EDGE
        rows = iota((EDGE, TILE), 0, F32)
        near = rows == coord_y
        far = rows == coord_y + 1.0
        x_full = jnp.broadcast_to(coord_x, (EDGE, TILE)).astype(BF16)
        none = jnp.zeros((EDGE, TILE), BF16)
        for e in range(2):
            parts = []
            for a in range(2):
                low = weight_ref[tile, (4 * a + e) * S + s : (4 * a + e) * S + s + 1, :]
                high = weight_ref[tile, (4 * a + 2 + e) * S + s : (4 * a + 2 + e) * S + s + 1, :]
                parts.append(jnp.where(near, low, jnp.where(far, high, 0.0)).astype(BF16))
            for x in range(EDGE):
                value = jnp.where(x_full == x, parts[0], none)
                if x > 0:
                    value = jnp.where(x_full == x - 1, parts[1], value)
                mix_ref[u, e * LINES + x * EDGE : e * LINES + (x + 1) * EDGE, lanes] = value

    def spread(tile, u, group):
        brick = (
            (tile >= limit1).astype(jnp.int32)
            + (tile >= limit2).astype(jnp.int32)
            + (tile >= limit3).astype(jnp.int32)
        )
        lanes = slice(group * WIDE, (group + 1) * WIDE)
        read = dot(brick_ref[brick], mix_ref[u, :, lanes])
        coord_z = jnp.concatenate(
            [feature_ref[tile, S + EACH * group + i : S + EACH * group + i + 1, :] for i in range(EACH)],
            axis=1,
        )
        mixed = jnp.zeros((CH, WIDE), F32)
        for p in range(POS):
            mixed = jnp.where(coord_z == float(p), read[p * CH : (p + 1) * CH], mixed)
        mixed_ref[u, :, lanes] = mixed.astype(BF16)

    def shade(u):
        layer = mixed_ref[u]
        for w_ref in (w_in_ref, w_mid_ref, w_last_ref):
            layer = jnp.maximum(dot(w_ref[...], layer), 0.0).astype(BF16)
        hidden_ref[u] = layer
        thin = dot(w_density_ref[...], layer)
        for s in range(S):
            density_ref[u, s : s + 1, :] = thin[0:1, s * TILE : (s + 1) * TILE]

    def composite(tile, u):
        density = density_ref[u]
        density = jnp.maximum(density, 0.0) + jnp.log1p(jnp.exp(-jnp.abs(density)))
        optical = density * feature_ref[tile, 2 * S : 3 * S, :]
        ahead = [jnp.zeros((1, TILE), F32)]
        for s in range(S):
            ahead.append(ahead[s] + optical[s : s + 1])
        clear = jnp.exp(-jnp.concatenate(ahead[:S], axis=0))
        share = clear * (1.0 - jnp.exp(-optical))
        total = jnp.zeros((HID, TILE), F32)
        for s in range(S):
            hidden = hidden_ref[u, :, s * TILE : (s + 1) * TILE].astype(F32)
            total = total + hidden * share[s : s + 1]
        high = total.astype(BF16)
        low = (total - high.astype(F32)).astype(BF16)
        colour = dot(w_feat_ref[...], high) + dot(w_feat_ref[...], low)
        thick = ahead[S]
        thick_high = thick.astype(BF16).astype(F32)
        thick_mid = (thick - thick_high).astype(BF16).astype(F32)
        thick_low = thick - thick_high - thick_mid
        extra = jnp.concatenate(
            [thick_high, thick_mid, thick_low, jnp.zeros((13, TILE), F32)], axis=0
        )
        result_ref[tile] = jnp.concatenate([colour, extra], axis=0).astype(BF16)

    for load in loads[1:]:
        load.wait()
    w_in_ref[...] = turned_ref[...].astype(F32).T.astype(BF16)
    w_density_ref[...] = jnp.broadcast_to(thin_ref[...].astype(F32), (16, HID)).astype(BF16)
    groups = S // EACH
    for s in range(S):
        build(0, 0, s)

    def two_tiles(step, carried):
        tile = 2 * step
        following = jnp.minimum(tile + 2, SPACE - 1)
        for group in range(groups):
            spread(tile, 0, group)
            for s in range(EACH):
                build(tile + 1, 1, group * EACH + s)
        shade(0)
        for group in range(groups):
            spread(tile + 1, 1, group)
            for s in range(EACH):
                build(following, 0, group * EACH + s)
            if group == groups // 2:
                composite(tile, 0)
        shade(1)
        composite(tile + 1, 1)
        return carried

    lax.fori_loop(0, lax.div(tile_count + 1, 2), two_tiles, 0)

    def scatter(step, carried):
        tiles = [step * GATHER + u for u in range(GATHER)]
        result = jnp.concatenate([result_ref[tile] for tile in tiles], axis=1)
        chosen = chosen_ref[pl.ds(step * GATHER, GATHER)].reshape(GATHER * TILE, SLOTS)
        reply_ref[...] += dot(result, chosen)
        return carried

    lax.fori_loop(0, lax.div(tile_count + GATHER - 1, GATHER), scatter, 0)
    for part in range(2):
        block = reply_ref[:HID, part * half : (part + 1) * half].T
        colour_ref[:, part * HALF : (part + 1) * HALF, :] = block.astype(BF16).reshape(
            COLS, HALF, HID
        )
    index = iota((1, SLOTS), 1, F32)
    part = jnp.floor(index * (1.0 / half))
    inside = index - part * half
    column = jnp.floor(inside * (1.0 / HALF))
    rank = inside - column * HALF + part * HALF
    columns = one_hot(iota((COLS, SLOTS), 0, F32) == column)
    ranks = iota((CAP, SLOTS), 0, F32) == rank
    spots = jnp.concatenate(
        [jnp.where(ranks, reply_ref[HID + i : HID + i + 1, :], 0.0) for i in range(4)], axis=0
    ).astype(BF16)
    depth = dot_rows(columns, spots)
    depth_ref[...] = depth.reshape(COLS, 1, HID)


def collect_kernel(
    colour_ref,
    depth_ref,
    place_ref,
    image_ref,
    visible_ref,
    got_ref,
    deep_ref,
    here_ref,
    thick_ref,
    colours_ref,
    thicks_ref,
    send_sem,
    recv_sem,
    local_sem,
    deep_send,
    deep_recv,
    deep_local,
    colour_send,
    colour_recv,
    thick_send,
    thick_recv,
):
    regions = lax.axis_size("depth")
    me = lax.axis_index("depth")
    barrier = pltpu.get_barrier_semaphore()
    greet(barrier, COLS)
    for step in range(1, regions):
        peer = lax.rem(me + step, regions)
        pl.semaphore_signal(barrier, inc=1, device_id={"depth": peer}, device_id_type=MESH)
    owner = place_ref[0:1, :]
    rank = place_ref[1:2, :]
    pl.semaphore_wait(barrier, COLS - 1 + regions - 1)
    start_exchange(depth_ref, deep_ref, deep_send, deep_recv, deep_local)
    start_exchange(colour_ref, got_ref, send_sem, recv_sem, local_sem)
    found = one_hot(iota((SLOTS, RAYS), 0) == owner * CAP + rank)
    end_exchange(depth_ref, deep_ref, deep_send, deep_recv, deep_local)
    mine = one_hot(iota((COLS, RAYS), 0) == owner)
    depth = deep_ref[...].reshape(COLS, HID)
    depth = dot(depth.T.astype(BF16), mine)
    ranks = iota((CAP, RAYS), 0) == rank
    thick = jnp.zeros((1, RAYS), F32)
    for i in range(3):
        piece = jnp.where(ranks, depth[i * CAP : (i + 1) * CAP], 0.0)
        thick = thick + jnp.sum(piece, axis=0, keepdims=True)
    thick_ref[...] = thick
    copies = []
    for step in range(1, regions):
        peer = lax.rem(me + step, regions)
        copy = pltpu.make_async_remote_copy(
            src_ref=thick_ref,
            dst_ref=thicks_ref.at[step],
            send_sem=thick_send.at[step],
            recv_sem=thick_recv.at[step],
            device_id={"depth": peer},
            device_id_type=MESH,
        )
        copy.start()
        copies.append(copy)
    end_exchange(colour_ref, got_ref, send_sem, recv_sem, local_sem)
    table = got_ref[...].reshape(SLOTS, HID).astype(F32).T.astype(BF16)
    rows = HID // regions
    here_ref[...] = dot(table, found).astype(BF16).reshape(regions, rows, RAYS)
    for step in range(1, regions):
        peer = lax.rem(me + step, regions)
        copy = pltpu.make_async_remote_copy(
            src_ref=here_ref.at[peer],
            dst_ref=colours_ref.at[step],
            send_sem=colour_send.at[step],
            recv_sem=colour_recv.at[step],
            device_id={"depth": peer},
            device_id_type=MESH,
        )
        copy.start()
        copies.append(copy)
    for copy in copies:
        copy.wait()
    parts = [thick] + [thicks_ref[step] for step in range(1, regions)]
    sources = [lax.rem(me - step + regions, regions) for step in range(regions)]
    image = jnp.zeros((rows, RAYS), F32)
    for step in range(regions):
        ahead = jnp.zeros((1, RAYS), F32)
        for other in range(regions):
            if other != step:
                front = (sources[other] < sources[step]).astype(F32)
                ahead = ahead + front * parts[other]
        visible = jnp.exp(-ahead)
        if step == 0:
            visible_ref[...] = visible
            colour = here_ref[me]
        else:
            colour = colours_ref[step]
        image = image + visible * colour.astype(F32)
    image_ref[...] = image


def hbm(count):
    return [pl.BlockSpec(memory_space=pltpu.HBM)] * count


def vmem(count):
    return [pl.BlockSpec(memory_space=pltpu.VMEM)] * count


def run_field(got, table, w_in, w_mid, w_last, w_feat, w_density):
    return pl.pallas_call(
        field_kernel,
        out_shape=(
            jax.ShapeDtypeStruct((COLS, CAP, HID), BF16),
            jax.ShapeDtypeStruct((COLS, 1, HID), F32),
        ),
        in_specs=hbm(7),
        out_specs=tuple(vmem(2)),
        scratch_shapes=[
            pltpu.VMEM(got.shape, BF16),
            pltpu.VMEM(table.shape, BF16),
            pltpu.VMEM((CH, HID), BF16),
            pltpu.VMEM((HID, CH), BF16),
            pltpu.VMEM((HID, HID), BF16),
            pltpu.VMEM((HID, HID), BF16),
            pltpu.VMEM((HID, HID), BF16),
            pltpu.VMEM((1, HID), BF16),
            pltpu.VMEM((16, HID), BF16),
            pltpu.SemaphoreType.DMA((7,)),
            pltpu.VMEM((SLOTS, 2 * HID), BF16),
            pltpu.VMEM((8, SLOTS), F32),
            pltpu.VMEM((SPACE, TILE, SLOTS), BF16),
            pltpu.VMEM((SPACE, HID, TILE), F32),
            pltpu.VMEM((SPACE, HID // 2, TILE), F32),
            pltpu.VMEM((BUFFERS, 2 * LINES, S * TILE), BF16),
            pltpu.VMEM((BUFFERS, CH, S * TILE), BF16),
            pltpu.VMEM((BUFFERS, HID, S * TILE), BF16),
            pltpu.VMEM((BUFFERS, S, TILE), F32),
            pltpu.VMEM((SPACE, HID + 16, TILE), BF16),
            pltpu.VMEM((HID + 16, SLOTS), F32),
        ],
        compiler_params=pltpu.CompilerParams(vmem_limit_bytes=58 << 20),
        name="field",
    )(got, table, w_in.T, w_mid, w_last, w_feat, w_density)


def on_device(
    bricks,
    brick_owner,
    brick_slot,
    sample_base,
    corner_weights,
    spacing,
    w_in,
    w_mid,
    w_last,
    w_feat,
    w_density,
):
    got, place, table = pl.pallas_call(
        ask_kernel,
        out_shape=(
            jax.ShapeDtypeStruct((COLS, ROWS, HID), BF16),
            jax.ShapeDtypeStruct((2, RAYS), jnp.int32),
            jax.ShapeDtypeStruct((bricks.shape[1], POS * CH, 2 * LINES), BF16),
        ),
        in_specs=hbm(6),
        out_specs=(hbm(1)[0], vmem(1)[0], hbm(1)[0]),
        scratch_shapes=[
            pltpu.VMEM((COLS, ROWS, HID), BF16),
            pltpu.VMEM((1, RAYS), jnp.int32),
            pltpu.VMEM((1, RAYS), jnp.int32),
            pltpu.VMEM((S, RAYS), jnp.int32),
            pltpu.VMEM((HID, RAYS), BF16),
            pltpu.VMEM((S, RAYS), BF16),
            pltpu.VMEM(bricks.shape[1:], BF16),
            pltpu.VMEM((bricks.shape[1], POS * CH, 2 * LINES), BF16),
            pltpu.SemaphoreType.DMA((6,)),
            pltpu.SemaphoreType.DMA,
            pltpu.SemaphoreType.DMA,
            pltpu.SemaphoreType.DMA,
            pltpu.SemaphoreType.DMA,
        ],
        compiler_params=pltpu.CompilerParams(
            vmem_limit_bytes=58 << 20, collective_id=0, has_side_effects=True
        ),
        name="ask",
    )(
        brick_owner.reshape(1, RAYS),
        brick_slot,
        sample_base[0],
        corner_weights[0].reshape(HID, RAYS),
        spacing[0],
        bricks[0],
    )
    colour, depth = run_field(got, table, w_in, w_mid, w_last, w_feat, w_density)
    regions = lax.axis_size("depth")
    rows = HID // regions
    return pl.pallas_call(
        collect_kernel,
        out_shape=(
            jax.ShapeDtypeStruct((rows, RAYS), F32),
            jax.ShapeDtypeStruct((1, RAYS), F32),
        ),
        in_specs=hbm(2) + vmem(1),
        out_specs=tuple(vmem(2)),
        scratch_shapes=[
            pltpu.VMEM((COLS, CAP, HID), BF16),
            pltpu.VMEM((COLS, 1, HID), F32),
            pltpu.VMEM((regions, rows, RAYS), BF16),
            pltpu.VMEM((1, RAYS), F32),
            pltpu.VMEM((regions, rows, RAYS), BF16),
            pltpu.VMEM((regions, 1, RAYS), F32),
            pltpu.SemaphoreType.DMA,
            pltpu.SemaphoreType.DMA,
            pltpu.SemaphoreType.DMA,
            pltpu.SemaphoreType.DMA,
            pltpu.SemaphoreType.DMA,
            pltpu.SemaphoreType.DMA,
            pltpu.SemaphoreType.DMA((regions,)),
            pltpu.SemaphoreType.DMA((regions,)),
            pltpu.SemaphoreType.DMA((regions,)),
            pltpu.SemaphoreType.DMA((regions,)),
        ],
        compiler_params=pltpu.CompilerParams(
            vmem_limit_bytes=58 << 20, collective_id=1, has_side_effects=True
        ),
        name="collect",
    )(colour, depth, place)


def solution(mesh):
    in_specs = (
        P("depth", "cols", None, None),
        P("depth", "cols", None),
        P("depth", "cols"),
        P("depth", None, "cols"),
        P("depth", None, None, "cols"),
        P("depth", None, "cols"),
        P(),
        P(),
        P(),
        P(),
        P(),
    )
    out_specs = (P("depth", "cols"), P("depth", "cols"))
    return jax.shard_map(
        on_device, mesh=mesh, in_specs=in_specs, out_specs=out_specs, check_vma=False
    )
```

```python
import jax
import jax.numpy as jnp
from jax import lax
from jax.experimental import pallas as pl
from jax.experimental.pallas import tpu as pltpu
from jax.sharding import PartitionSpec as P

EDGE = 16
LINES = EDGE * EDGE
CH = 32
S = 16
HID = 128
COLS = 64
CAP = 32
HALF = CAP // 2
ROWS = 48
RAYS = 1024
SLOTS = COLS * CAP
TILE = 128
MAX_TILES = SLOTS // TILE + 3
POS = EDGE - 1
WIDE = 256
EACH = WIDE // TILE
GATHER = 4
SPACE = MAX_TILES + 1
BUFFERS = 2
F32 = jnp.float32
BF16 = jnp.bfloat16
MESH = pl.DeviceIdType.MESH


def iota(shape, dim, dtype=jnp.int32):
    return lax.broadcasted_iota(jnp.int32, shape, dim).astype(dtype)


def one_hot(mask):
    return jnp.where(mask, 1.0, 0.0).astype(BF16)


def dot(a, b):
    return jnp.dot(a, b, preferred_element_type=F32)


def dot_rows(a, b):
    return lax.dot_general(a, b, (((1,), (1,)), ((), ())), preferred_element_type=F32)


def greet(barrier, count):
    me = lax.axis_index("cols")

    def signal(step, carried):
        peer = lax.rem(me + step, count)
        pl.semaphore_signal(barrier, inc=1, device_id={"cols": peer}, device_id_type=MESH)
        return carried

    lax.fori_loop(1, count, signal, 0)


def start_exchange(from_ref, to_ref, send_sem, recv_sem, local_sem):
    me = lax.axis_index("cols")

    def send(step, carried):
        peer = lax.rem(me + step, COLS)
        pltpu.make_async_remote_copy(
            src_ref=from_ref.at[peer],
            dst_ref=to_ref.at[me],
            send_sem=send_sem,
            recv_sem=recv_sem,
            device_id={"cols": peer},
            device_id_type=MESH,
        ).start()
        return carried

    lax.fori_loop(1, COLS, send, 0)
    pltpu.make_async_copy(from_ref.at[me], to_ref.at[me], local_sem).start()


def end_exchange(from_ref, to_ref, send_sem, recv_sem, local_sem):
    me = lax.axis_index("cols")
    others = pl.ds(0, COLS - 1)
    pltpu.make_async_copy(from_ref.at[me], to_ref.at[me], local_sem).wait()
    pltpu.make_async_copy(from_ref.at[others], from_ref.at[others], send_sem).wait()
    pltpu.make_async_copy(to_ref.at[others], to_ref.at[others], recv_sem).wait()


def ask_kernel(
    owner_hbm,
    slot_hbm,
    base_hbm,
    weight_hbm,
    spacing_hbm,
    brick_hbm,
    got_ref,
    place_ref,
    table_hbm,
    sent_ref,
    owner_ref,
    slot_ref,
    base_ref,
    weight_ref,
    spacing_ref,
    brick_ref,
    table_ref,
    load_sem,
    table_sem,
    send_sem,
    recv_sem,
    local_sem,
):
    loads = [
        pltpu.make_async_copy(source, target, load_sem.at[i])
        for i, (source, target) in enumerate(
            (
                (owner_hbm, owner_ref),
                (slot_hbm, slot_ref),
                (base_hbm, base_ref),
                (weight_hbm, weight_ref),
                (spacing_hbm, spacing_ref),
                (brick_hbm, brick_ref),
            )
        )
    ]
    for load in loads:
        load.start()
    barrier = pltpu.get_barrier_semaphore()
    greet(barrier, COLS)
    for load in loads[:5]:
        load.wait()
    owner = owner_ref[...]
    mine = iota((COLS, RAYS), 0) == owner
    earlier = one_hot(iota((RAYS, RAYS), 0) < iota((RAYS, RAYS), 1))
    count = dot(one_hot(mine), earlier)
    rank = jnp.sum(jnp.where(mine, count, 0.0), axis=0, keepdims=True).astype(jnp.int32)
    place = owner * CAP + rank
    place_ref[...] = jnp.concatenate([owner, rank], axis=0)
    sent = dot_rows(one_hot(iota((SLOTS, RAYS), 0) == place), weight_ref[...])
    sent_ref[:, :CAP, :] = sent.astype(BF16).reshape(COLS, CAP, HID)
    base = base_ref[...].astype(F32) + 0.5
    side = EDGE - 1
    coord_x = jnp.floor(base * (1.0 / (side * side)))
    rest = base - coord_x * (side * side)
    coord_y = jnp.floor(rest * (1.0 / side))
    coord_z = rest - coord_y * side - 0.5
    line = coord_x * EDGE + coord_y
    slot = slot_ref[...].astype(F32) + 1.0
    slot_rows = jnp.where(iota((S, RAYS), 0) == 0, slot, 0.0)
    features = jnp.concatenate([line, coord_z, spacing_ref[...].astype(F32), slot_rows], axis=0)
    second = rank >= HALF
    both = jnp.concatenate(
        [jnp.where(second, 0.0, features), jnp.where(second, features, 0.0)], axis=0
    ).astype(BF16)
    row = owner * HALF + jnp.where(second, rank - HALF, rank)
    sent = dot_rows(one_hot(iota((COLS * HALF, RAYS), 0) == row), both)
    sent_ref[:, CAP:, :] = sent.astype(BF16).reshape(COLS, HALF, HID)
    pl.semaphore_wait(barrier, COLS - 1)
    start_exchange(sent_ref, got_ref, send_sem, recv_sem, local_sem)
    loads[5].wait()
    for q in range(brick_ref.shape[0]):
        turned = brick_ref[q].astype(F32).T.astype(BF16)
        table_ref[q, :, :LINES] = turned[: POS * CH]
        table_ref[q, :, LINES:] = turned[CH:]
    store = pltpu.make_async_copy(table_ref, table_hbm, table_sem)
    store.start()
    store.wait()
    end_exchange(sent_ref, got_ref, send_sem, recv_sem, local_sem)


def field_kernel(
    got_hbm,
    brick_hbm,
    w_in_hbm,
    w_mid_hbm,
    w_last_hbm,
    w_feat_hbm,
    w_density_hbm,
    colour_ref,
    depth_ref,
    got_ref,
    brick_ref,
    turned_ref,
    w_in_ref,
    w_mid_ref,
    w_last_ref,
    w_feat_ref,
    thin_ref,
    w_density_ref,
    load_sem,
    table_ref,
    pos_ref,
    chosen_ref,
    weight_ref,
    feature_ref,
    mix_ref,
    mixed_ref,
    hidden_ref,
    density_ref,
    result_ref,
    reply_ref,
):
    loads = [
        pltpu.make_async_copy(source, target, load_sem.at[i])
        for i, (source, target) in enumerate(
            (
                (got_hbm, got_ref),
                (brick_hbm, brick_ref),
                (w_in_hbm, turned_ref),
                (w_mid_hbm, w_mid_ref),
                (w_last_hbm, w_last_ref),
                (w_feat_hbm, w_feat_ref),
                (w_density_hbm, thin_ref),
            )
        )
    ]
    for load in loads:
        load.start()
    loads[0].wait()
    half = COLS * HALF
    second = got_ref[:, CAP:, :].reshape(half, HID)
    lane = iota((half, HID), 1)
    table_ref[:half, :HID] = got_ref[:, :HALF, :].reshape(half, HID)
    table_ref[half:, :HID] = got_ref[:, HALF:CAP, :].reshape(half, HID)
    zero = jnp.zeros((half, HID), BF16)
    table_ref[:half, HID:] = jnp.where(lane < HID // 2, second, zero)
    table_ref[half:, HID:] = jnp.where(lane < HID // 2, zero, second)

    pick_row = iota((16, HID), 0)
    pick_lane = iota((16, HID), 1)
    picks = one_hot(pick_lane == jnp.where(pick_row < 2, 3 * S + pick_row * (HID // 2), -1))
    keys = dot_rows(picks, second)
    key = jnp.concatenate([keys[0:1], keys[1:2]], axis=1) - 1.0
    member = jnp.where(iota((8, SLOTS), 0, F32) == key, 1.0, 0.0)
    chunks = SLOTS // 128
    stacked = jnp.concatenate([member[:, c * 128 : (c + 1) * 128] for c in range(chunks)], axis=0)
    before = one_hot(iota((128, 128), 0) < iota((128, 128), 1))
    inner = dot(stacked.astype(BF16), before)
    totals = jnp.sum(stacked, axis=1, keepdims=True)
    carry = jnp.zeros((8, 1), F32)
    pieces = []
    for c in range(chunks):
        pieces.append(inner[c * 8 : (c + 1) * 8] + carry)
        carry = carry + totals[c * 8 : (c + 1) * 8]
    counted = jnp.concatenate(pieces, axis=1)
    tiles = jnp.floor((carry + (TILE - 1.0)) * (1.0 / TILE))
    row = iota((8, 1), 0)
    starts = [jnp.sum(jnp.where(row < q, tiles, 0.0)) for q in range(1, 5)]
    first = jnp.where(row == 1, starts[0], jnp.where(row == 2, starts[1], starts[2]))
    first = jnp.where(row == 0, 0.0, first)
    pos = jnp.sum(member * (counted + first * TILE), axis=0, keepdims=True)
    pos = jnp.where(jnp.sum(member, axis=0, keepdims=True) > 0.0, pos, -1.0)
    pos_ref[...] = jnp.broadcast_to(pos, (8, SLOTS))
    limit1, limit2, limit3, tile_count = [start.astype(jnp.int32) for start in starts]
    reply_ref[...] = jnp.zeros_like(reply_ref)
    result_ref[...] = jnp.zeros_like(result_ref)

    def gather(step, carried):
        for u in range(GATHER):
            tile = step * GATHER + u
            local = pos_ref[0:1, :] - (tile * TILE).astype(F32)
            chosen_ref[tile] = one_hot(iota((TILE, SLOTS), 0, F32) == local)
        chosen = chosen_ref[pl.ds(step * GATHER, GATHER)].reshape(GATHER * TILE, SLOTS)
        rays = dot(chosen, table_ref[...])
        for u in range(GATHER):
            turned = rays[u * TILE : (u + 1) * TILE].T
            weight_ref[step * GATHER + u] = turned[:HID]
            feature_ref[step * GATHER + u] = turned[HID : HID + HID // 2] + turned[HID + HID // 2 :]
        return carried

    lax.fori_loop(0, lax.div(tile_count + GATHER - 1, GATHER), gather, 0)

    def build(tile, u, s):
        lanes = slice(s * TILE, (s + 1) * TILE)
        line = feature_ref[tile, s : s + 1, :]
        coord_x = jnp.floor(line * (1.0 / EDGE))
        coord_y = line - coord_x * EDGE
        rows = iota((EDGE, TILE), 0, F32)
        near = rows == coord_y
        far = rows == coord_y + 1.0
        x_full = jnp.broadcast_to(coord_x, (EDGE, TILE)).astype(BF16)
        none = jnp.zeros((EDGE, TILE), BF16)
        for e in range(2):
            parts = []
            for a in range(2):
                low = weight_ref[tile, (4 * a + e) * S + s : (4 * a + e) * S + s + 1, :]
                high = weight_ref[tile, (4 * a + 2 + e) * S + s : (4 * a + 2 + e) * S + s + 1, :]
                parts.append(jnp.where(near, low, jnp.where(far, high, 0.0)).astype(BF16))
            for x in range(EDGE):
                value = jnp.where(x_full == x, parts[0], none)
                if x > 0:
                    value = jnp.where(x_full == x - 1, parts[1], value)
                mix_ref[u, e * LINES + x * EDGE : e * LINES + (x + 1) * EDGE, lanes] = value

    def spread(tile, u, group):
        brick = (
            (tile >= limit1).astype(jnp.int32)
            + (tile >= limit2).astype(jnp.int32)
            + (tile >= limit3).astype(jnp.int32)
        )
        lanes = slice(group * WIDE, (group + 1) * WIDE)
        read = dot(brick_ref[brick], mix_ref[u, :, lanes])
        coord_z = jnp.concatenate(
            [feature_ref[tile, S + EACH * group + i : S + EACH * group + i + 1, :] for i in range(EACH)],
            axis=1,
        )
        mixed = jnp.zeros((CH, WIDE), F32)
        for p in range(POS):
            mixed = jnp.where(coord_z == float(p), read[p * CH : (p + 1) * CH], mixed)
        mixed_ref[:, slice(u * S * TILE + group * WIDE, u * S * TILE + (group + 1) * WIDE)] = mixed.astype(BF16)

    def shade():
        layer = mixed_ref[...]
        for w_ref in (w_in_ref, w_mid_ref, w_last_ref):
            layer = jnp.maximum(dot(w_ref[...], layer), 0.0).astype(BF16)
        hidden_ref[...] = layer
        thin = dot(w_density_ref[...], layer)
        for u in range(BUFFERS):
            for s in range(S):
                start = (u * S + s) * TILE
                density_ref[u, s : s + 1, :] = thin[0:1, start : start + TILE]

    def composite(tile, u):
        density = density_ref[u]
        density = jnp.maximum(density, 0.0) + jnp.log1p(jnp.exp(-jnp.abs(density)))
        optical = density * feature_ref[tile, 2 * S : 3 * S, :]
        ahead = [jnp.zeros((1, TILE), F32)]
        for s in range(S):
            ahead.append(ahead[s] + optical[s : s + 1])
        clear = jnp.exp(-jnp.concatenate(ahead[:S], axis=0))
        share = clear * (1.0 - jnp.exp(-optical))
        total = jnp.zeros((HID, TILE), F32)
        for s in range(S):
            start = (u * S + s) * TILE
            hidden = hidden_ref[:, start : start + TILE].astype(F32)
            total = total + hidden * share[s : s + 1]
        high = total.astype(BF16)
        low = (total - high.astype(F32)).astype(BF16)
        colour = dot(w_feat_ref[...], high) + dot(w_feat_ref[...], low)
        thick = ahead[S]
        thick_high = thick.astype(BF16).astype(F32)
        thick_mid = (thick - thick_high).astype(BF16).astype(F32)
        thick_low = thick - thick_high - thick_mid
        extra = jnp.concatenate(
            [thick_high, thick_mid, thick_low, jnp.zeros((13, TILE), F32)], axis=0
        )
        result_ref[tile] = jnp.concatenate([colour, extra], axis=0).astype(BF16)

    for load in loads[1:]:
        load.wait()
    w_in_ref[...] = turned_ref[...].astype(F32).T.astype(BF16)
    w_density_ref[...] = jnp.broadcast_to(thin_ref[...].astype(F32), (16, HID)).astype(BF16)
    groups = S // EACH
    for s in range(S):
        build(0, 0, s)

    def two_tiles(step, carried):
        tile = 2 * step
        following = jnp.minimum(tile + 2, SPACE - 1)
        for group in range(groups):
            spread(tile, 0, group)
            for s in range(EACH):
                build(tile + 1, 1, group * EACH + s)
        for group in range(groups):
            spread(tile + 1, 1, group)
            for s in range(EACH):
                build(following, 0, group * EACH + s)
        shade()
        composite(tile, 0)
        composite(tile + 1, 1)
        return carried

    lax.fori_loop(0, lax.div(tile_count + 1, 2), two_tiles, 0)

    def scatter(step, carried):
        tiles = [step * GATHER + u for u in range(GATHER)]
        result = jnp.concatenate([result_ref[tile] for tile in tiles], axis=1)
        chosen = chosen_ref[pl.ds(step * GATHER, GATHER)].reshape(GATHER * TILE, SLOTS)
        reply_ref[...] += dot(result, chosen)
        return carried

    lax.fori_loop(0, lax.div(tile_count + GATHER - 1, GATHER), scatter, 0)
    for part in range(2):
        block = reply_ref[:HID, part * half : (part + 1) * half].T
        colour_ref[:, part * HALF : (part + 1) * HALF, :] = block.astype(BF16).reshape(
            COLS, HALF, HID
        )
    index = iota((1, SLOTS), 1, F32)
    part = jnp.floor(index * (1.0 / half))
    inside = index - part * half
    column = jnp.floor(inside * (1.0 / HALF))
    rank = inside - column * HALF + part * HALF
    columns = one_hot(iota((COLS, SLOTS), 0, F32) == column)
    ranks = iota((CAP, SLOTS), 0, F32) == rank
    spots = jnp.concatenate(
        [jnp.where(ranks, reply_ref[HID + i : HID + i + 1, :], 0.0) for i in range(4)], axis=0
    ).astype(BF16)
    depth = dot_rows(columns, spots)
    depth_ref[...] = depth.reshape(COLS, 1, HID)


def collect_kernel(
    colour_ref,
    depth_ref,
    place_ref,
    image_ref,
    visible_ref,
    got_ref,
    deep_ref,
    here_ref,
    thick_ref,
    colours_ref,
    thicks_ref,
    send_sem,
    recv_sem,
    local_sem,
    deep_send,
    deep_recv,
    deep_local,
    colour_send,
    colour_recv,
    thick_send,
    thick_recv,
):
    regions = lax.axis_size("depth")
    me = lax.axis_index("depth")
    barrier = pltpu.get_barrier_semaphore()
    greet(barrier, COLS)
    for step in range(1, regions):
        peer = lax.rem(me + step, regions)
        pl.semaphore_signal(barrier, inc=1, device_id={"depth": peer}, device_id_type=MESH)
    owner = place_ref[0:1, :]
    rank = place_ref[1:2, :]
    pl.semaphore_wait(barrier, COLS - 1 + regions - 1)
    start_exchange(depth_ref, deep_ref, deep_send, deep_recv, deep_local)
    start_exchange(colour_ref, got_ref, send_sem, recv_sem, local_sem)
    found = one_hot(iota((SLOTS, RAYS), 0) == owner * CAP + rank)
    end_exchange(depth_ref, deep_ref, deep_send, deep_recv, deep_local)
    mine = one_hot(iota((COLS, RAYS), 0) == owner)
    depth = deep_ref[...].reshape(COLS, HID)
    depth = dot(depth.T.astype(BF16), mine)
    ranks = iota((CAP, RAYS), 0) == rank
    thick = jnp.zeros((1, RAYS), F32)
    for i in range(3):
        piece = jnp.where(ranks, depth[i * CAP : (i + 1) * CAP], 0.0)
        thick = thick + jnp.sum(piece, axis=0, keepdims=True)
    thick_ref[...] = thick
    copies = []
    for step in range(1, regions):
        peer = lax.rem(me + step, regions)
        copy = pltpu.make_async_remote_copy(
            src_ref=thick_ref,
            dst_ref=thicks_ref.at[step],
            send_sem=thick_send.at[step],
            recv_sem=thick_recv.at[step],
            device_id={"depth": peer},
            device_id_type=MESH,
        )
        copy.start()
        copies.append(copy)
    end_exchange(colour_ref, got_ref, send_sem, recv_sem, local_sem)
    table = got_ref[...].reshape(SLOTS, HID).astype(F32).T.astype(BF16)
    rows = HID // regions
    here_ref[...] = dot(table, found).astype(BF16).reshape(regions, rows, RAYS)
    for step in range(1, regions):
        peer = lax.rem(me + step, regions)
        copy = pltpu.make_async_remote_copy(
            src_ref=here_ref.at[peer],
            dst_ref=colours_ref.at[step],
            send_sem=colour_send.at[step],
            recv_sem=colour_recv.at[step],
            device_id={"depth": peer},
            device_id_type=MESH,
        )
        copy.start()
        copies.append(copy)
    for copy in copies:
        copy.wait()
    parts = [thick] + [thicks_ref[step] for step in range(1, regions)]
    sources = [lax.rem(me - step + regions, regions) for step in range(regions)]
    image = jnp.zeros((rows, RAYS), F32)
    for step in range(regions):
        ahead = jnp.zeros((1, RAYS), F32)
        for other in range(regions):
            if other != step:
                front = (sources[other] < sources[step]).astype(F32)
                ahead = ahead + front * parts[other]
        visible = jnp.exp(-ahead)
        if step == 0:
            visible_ref[...] = visible
            colour = here_ref[me]
        else:
            colour = colours_ref[step]
        image = image + visible * colour.astype(F32)
    image_ref[...] = image


def hbm(count):
    return [pl.BlockSpec(memory_space=pltpu.HBM)] * count


def vmem(count):
    return [pl.BlockSpec(memory_space=pltpu.VMEM)] * count


def run_field(got, table, w_in, w_mid, w_last, w_feat, w_density):
    return pl.pallas_call(
        field_kernel,
        out_shape=(
            jax.ShapeDtypeStruct((COLS, CAP, HID), BF16),
            jax.ShapeDtypeStruct((COLS, 1, HID), F32),
        ),
        in_specs=hbm(7),
        out_specs=tuple(vmem(2)),
        scratch_shapes=[
            pltpu.VMEM(got.shape, BF16),
            pltpu.VMEM(table.shape, BF16),
            pltpu.VMEM((CH, HID), BF16),
            pltpu.VMEM((HID, CH), BF16),
            pltpu.VMEM((HID, HID), BF16),
            pltpu.VMEM((HID, HID), BF16),
            pltpu.VMEM((HID, HID), BF16),
            pltpu.VMEM((1, HID), BF16),
            pltpu.VMEM((16, HID), BF16),
            pltpu.SemaphoreType.DMA((7,)),
            pltpu.VMEM((SLOTS, 2 * HID), BF16),
            pltpu.VMEM((8, SLOTS), F32),
            pltpu.VMEM((SPACE, TILE, SLOTS), BF16),
            pltpu.VMEM((SPACE, HID, TILE), F32),
            pltpu.VMEM((SPACE, HID // 2, TILE), F32),
            pltpu.VMEM((BUFFERS, 2 * LINES, S * TILE), BF16),
            pltpu.VMEM((CH, BUFFERS * S * TILE), BF16),
            pltpu.VMEM((HID, BUFFERS * S * TILE), BF16),
            pltpu.VMEM((BUFFERS, S, TILE), F32),
            pltpu.VMEM((SPACE, HID + 16, TILE), BF16),
            pltpu.VMEM((HID + 16, SLOTS), F32),
        ],
        compiler_params=pltpu.CompilerParams(vmem_limit_bytes=58 << 20),
        name="field",
    )(got, table, w_in.T, w_mid, w_last, w_feat, w_density)


def on_device(
    bricks,
    brick_owner,
    brick_slot,
    sample_base,
    corner_weights,
    spacing,
    w_in,
    w_mid,
    w_last,
    w_feat,
    w_density,
):
    got, place, table = pl.pallas_call(
        ask_kernel,
        out_shape=(
            jax.ShapeDtypeStruct((COLS, ROWS, HID), BF16),
            jax.ShapeDtypeStruct((2, RAYS), jnp.int32),
            jax.ShapeDtypeStruct((bricks.shape[1], POS * CH, 2 * LINES), BF16),
        ),
        in_specs=hbm(6),
        out_specs=(hbm(1)[0], vmem(1)[0], hbm(1)[0]),
        scratch_shapes=[
            pltpu.VMEM((COLS, ROWS, HID), BF16),
            pltpu.VMEM((1, RAYS), jnp.int32),
            pltpu.VMEM((1, RAYS), jnp.int32),
            pltpu.VMEM((S, RAYS), jnp.int32),
            pltpu.VMEM((HID, RAYS), BF16),
            pltpu.VMEM((S, RAYS), BF16),
            pltpu.VMEM(bricks.shape[1:], BF16),
            pltpu.VMEM((bricks.shape[1], POS * CH, 2 * LINES), BF16),
            pltpu.SemaphoreType.DMA((6,)),
            pltpu.SemaphoreType.DMA,
            pltpu.SemaphoreType.DMA,
            pltpu.SemaphoreType.DMA,
            pltpu.SemaphoreType.DMA,
        ],
        compiler_params=pltpu.CompilerParams(
            vmem_limit_bytes=58 << 20, collective_id=0, has_side_effects=True
        ),
        name="ask",
    )(
        brick_owner.reshape(1, RAYS),
        brick_slot,
        sample_base[0],
        corner_weights[0].reshape(HID, RAYS),
        spacing[0],
        bricks[0],
    )
    colour, depth = run_field(got, table, w_in, w_mid, w_last, w_feat, w_density)
    regions = lax.axis_size("depth")
    rows = HID // regions
    return pl.pallas_call(
        collect_kernel,
        out_shape=(
            jax.ShapeDtypeStruct((rows, RAYS), F32),
            jax.ShapeDtypeStruct((1, RAYS), F32),
        ),
        in_specs=hbm(2) + vmem(1),
        out_specs=tuple(vmem(2)),
        scratch_shapes=[
            pltpu.VMEM((COLS, CAP, HID), BF16),
            pltpu.VMEM((COLS, 1, HID), F32),
            pltpu.VMEM((regions, rows, RAYS), BF16),
            pltpu.VMEM((1, RAYS), F32),
            pltpu.VMEM((regions, rows, RAYS), BF16),
            pltpu.VMEM((regions, 1, RAYS), F32),
            pltpu.SemaphoreType.DMA,
            pltpu.SemaphoreType.DMA,
            pltpu.SemaphoreType.DMA,
            pltpu.SemaphoreType.DMA,
            pltpu.SemaphoreType.DMA,
            pltpu.SemaphoreType.DMA,
            pltpu.SemaphoreType.DMA((regions,)),
            pltpu.SemaphoreType.DMA((regions,)),
            pltpu.SemaphoreType.DMA((regions,)),
            pltpu.SemaphoreType.DMA((regions,)),
        ],
        compiler_params=pltpu.CompilerParams(
            vmem_limit_bytes=56098816, collective_id=1, has_side_effects=True
        ),
        name="collect",
    )(colour, depth, place)


def solution(mesh):
    in_specs = (
        P("depth", "cols", None, None),
        P("depth", "cols", None),
        P("depth", "cols"),
        P("depth", None, "cols"),
        P("depth", None, None, "cols"),
        P("depth", None, "cols"),
        P(),
        P(),
        P(),
        P(),
        P(),
    )
    out_specs = (P("depth", "cols"), P("depth", "cols"))
    return jax.shard_map(
        on_device, mesh=mesh, in_specs=in_specs, out_specs=out_specs, check_vma=False
    )
```
